32 devices in a mesh: dp: 4 (over y, core), item: 8 (over z, x).
Axes of the slice: x: 2, y: 2, z: 4, core: 2. Of those that a mesh axis runs over, the one named last changes fastest.
Arguments:
- query: bfloat16 [32, 256], P(('dp', 'item')), may hold values from -40 to 40
- item_table: bfloat16 [65536, 256], P(('dp', 'item')), may hold values from -2.5 to 2.5
- context_features: bfloat16 [32, 512], P(('dp', 'item')), may hold values from -6 to 6
- candidates: int32 [32, 1024], P(('dp', 'item')), may hold values from 0 to 65535, as said below
- lengths: int32 [32], P(('dp', 'item')), may hold values from 128 to 1024, as said below
- logged_slot: int32 [32], P(('dp', 'item')), may hold values from 0 to 1023, as said below
- logging_prop: int32 [32], P(('dp', 'item')), may hold values from 256 to 4095
- w_first: bfloat16 [768, 512], replicated, may hold values from -0.21875 to 0.21875
- w_second: bfloat16 [512, 512], replicated, may hold values from -0.25 to 0.25
- w_score: bfloat16 [512], replicated, may hold values from -0.5 to 0.5
Outputs:
- section_logp: float32 [32, 1024], P(('dp', 'item'))
- log_weight: float32 [32], P(('dp', 'item'))
The draws below stay inside these ranges and needn't reach their ends.
Inputs may be any that keep to these rules, and one draw needn't show every extreme that they name: `candidates`: item ids. Among the 1024 candidate slots held by one device (its single context), at most 48 name items of any one block of 2048 consecutive ids, and for every device some block is named exactly 48 times. `lengths`: some context's list has 1024 live slots and some context's list has 128. `logged_slot`: below the context's length; the context with the longest list logs its last slot.
All inputs are finite; a program needn't handle non-finite values.
Results may differ from the reference program's by a relative error of at most 0.0003.
Values may be sent and summed in bfloat16 or wider, within the bound.
A program may use at most 64 MiB of HBM per device.

```python
import math
import jax
import jax.numpy as jnp
from jax import lax

D = 256
CF = 512
H = 512
ITEM_DEV = 2048
CTX_DEV = 1
CAND_MAX = 1024
MIN_LEN = 128
CTX = 32
ITEMS = 65536
CAP = 48
DEVICES = 32


def table_row(base_key, index):
    row_key = jax.random.fold_in(base_key, index)
    raw = jax.random.truncated_normal(row_key, -6.0, 6.0, (D,), jnp.float32)
    level = jax.random.uniform(jax.random.fold_in(row_key, 7), (), jnp.float32, 0.0, 1.0)
    spread = jnp.exp(level * jnp.log(jnp.float32(3.0))) * 2.0 / jnp.sqrt(jnp.float32(D))
    return jnp.clip(raw * spread, -2.5, 2.5)


def draw_item_table(key, part):
    base_key = jax.random.fold_in(key, 101)
    indices = jnp.arange(ITEMS, dtype=jnp.int32)
    rows = jax.vmap(lambda index: table_row(base_key, index))(indices)
    return rows.astype(jnp.bfloat16)


def draw_query(key, part):
    entries = jax.random.truncated_normal(jax.random.fold_in(key, 202), -6.0, 6.0, (CTX, D), jnp.float32)
    return entries.astype(jnp.bfloat16)


def draw_candidates(key, part):
    block_count = CTX // CTX_DEV
    slot_count = CTX_DEV * CAND_MAX

    def one_block(block_key):
        keys = jax.random.split(block_key, 4)
        leader = jax.random.randint(keys[0], (), 0, block_count)
        others = CAP + jax.random.permutation(keys[1], block_count * CAP - CAP)[:slot_count - CAP]
        picked = jnp.concatenate([jnp.arange(CAP, dtype=jnp.int32), others.astype(jnp.int32)])
        holder = (leader + picked // CAP) % block_count
        holder = holder[jax.random.permutation(keys[2], slot_count)]
        inside = jax.random.randint(keys[3], (slot_count,), 0, ITEM_DEV)
        return (holder * ITEM_DEV + inside).reshape(CTX_DEV, CAND_MAX)
    keys = jax.random.split(jax.random.fold_in(key, 303), block_count)
    return jax.vmap(one_block)(keys).reshape(CTX, CAND_MAX).astype(jnp.int32)


def longest_index(key):
    keys = jax.random.split(jax.random.fold_in(key, 404), 2)
    return jax.random.randint(keys[1], (), 0, CTX)


def list_lengths(key):
    keys = jax.random.split(jax.random.fold_in(key, 404), 1)
    drawn = jax.random.randint(keys[0], (CTX,), MIN_LEN, CAND_MAX + 1)
    longest = longest_index(key)
    shortest = (longest + 1) % CTX
    drawn = drawn.at[shortest].set(MIN_LEN)
    return drawn.at[longest].set(CAND_MAX).astype(jnp.int32)


def draw_lengths(key, part):
    return list_lengths(key)


def draw_logged_slot(key, part):
    list_len = list_lengths(key)
    drawn = jax.random.randint(jax.random.fold_in(key, 505), (CTX,), 0, 1 << 20)
    slots = drawn % list_len
    longest = longest_index(key)
    shortest = (longest + 1) % CTX
    slots = slots.at[shortest].set(0)
    slots = slots.at[longest].set(CAND_MAX - 1)
    return slots.astype(jnp.int32)


def touch_ends(result, own_key, smallest, largest):
    extent = result.shape
    spot = [jax.random.randint(jax.random.fold_in(own_key, axis), (), 0, extent[axis]) for axis in range(len(extent))]
    result = result.at[tuple(spot)].set(smallest)
    longest = extent.index(max(extent))
    spot[longest] = (spot[longest] + 1) % extent[longest]
    return result.at[tuple(spot)].set(largest)


def shard_levels(rng, shape, cuts, low, high):
    level, own = 1.0, jax.random.fold_in(rng, 6)
    for position, blocks in cuts:
        steps = jnp.exp(jax.random.uniform(jax.random.fold_in(own, position), (blocks,), jnp.float32, low / len(cuts), high / len(cuts)))
        level = level * jnp.repeat(steps, shape[position] // blocks).reshape([-1 if axis == position else 1 for axis in range(len(shape))])
    return level


def centred(stream_key, shape, deviation, bound, pieces=(), kind=jnp.bfloat16):
    values = jax.random.normal(stream_key, shape, jnp.float32) * deviation
    if len(pieces) > 0:
        values = shard_levels(stream_key, shape, pieces, -0.22, 0.18) * values
    return jnp.clip(values, min=-bound, max=bound).astype(kind)


def setup_inputs(seed: int = 0) -> dict:
    streams_of = jax.random.split(jax.random.key(seed), 11)
    query = draw_query(jax.random.fold_in(streams_of[10], 71), 0)
    item_table = draw_item_table(jax.random.fold_in(streams_of[10], 71), 0)
    context_features = centred(streams_of[2], (CTX, CF), 1.0, 6.0, ((0, 32),))
    candidates = draw_candidates(jax.random.fold_in(streams_of[10], 71), 0)
    lengths = draw_lengths(jax.random.fold_in(streams_of[10], 71), 0)
    logged_slot = draw_logged_slot(jax.random.fold_in(streams_of[10], 71), 0)
    logging_prop = touch_ends(jax.random.randint(streams_of[6], (CTX,), 256, 4096), jax.random.fold_in(streams_of[6], 1), 256, 4095).astype(jnp.int32)
    w_first = centred(streams_of[7], (CF + D, H), (CF + D) ** -0.5, 0.21875)
    w_second = centred(streams_of[8], (H, H), H ** -0.5, 0.25)
    w_score = centred(streams_of[9], (H,), 128 ** -0.5, 0.5)
    return {"query": query, "item_table": item_table, "context_features": context_features, "candidates": candidates, "lengths": lengths, "logged_slot": logged_slot, "logging_prop": logging_prop, "w_first": w_first, "w_second": w_second, "w_score": w_score}


def reference(query, item_table, context_features, candidates, lengths, logged_slot, logging_prop, w_first, w_second, w_score):
    slabs = item_table.reshape(DEVICES, ITEM_DEV, D)

    def sweep(running, slab_rows):
        running_max, running_sum = running
        logits = jnp.dot(query, slab_rows.T, preferred_element_type=jnp.float32)
        new_max = jnp.maximum(running_max, jnp.max(logits, axis=1))
        new_sum = running_sum * jnp.exp(running_max - new_max) + jnp.sum(jnp.exp(logits - new_max[:, None]), axis=1)
        return (new_max, new_sum), None

    initial = (jnp.full((CTX,), -1e30, jnp.float32), jnp.zeros((CTX,), jnp.float32))
    (running_max, running_sum), unused_out = lax.scan(sweep, initial, slabs)
    log_norm = running_max + jnp.log(running_sum)
    positions = jnp.arange(CAND_MAX, dtype=jnp.int32)

    def per_context(packed):
        query_row, feature_row, item_ids, list_length, norm_value, logged_index, propensity = packed
        cand_rows = item_table[item_ids]
        gen_logit = jnp.dot(cand_rows, query_row, preferred_element_type=jnp.float32)
        context_part = jnp.dot(feature_row[None, :], w_first[:CF], preferred_element_type=jnp.float32)
        item_part = jnp.dot(cand_rows, w_first[CF:], preferred_element_type=jnp.float32)
        hidden = jax.nn.silu(item_part + context_part).astype(jnp.bfloat16)
        second = jax.nn.silu(jnp.dot(hidden, w_second, preferred_element_type=jnp.float32)).astype(jnp.bfloat16)
        score = jnp.dot(second, w_score, preferred_element_type=jnp.float32)
        live_slots = positions < list_length
        masked = jnp.where(live_slots, score, jnp.float32(-1e30))
        rank_peak = jnp.max(masked)
        rank_norm = rank_peak + jnp.log(jnp.sum(jnp.where(live_slots, jnp.exp(masked - rank_peak), jnp.float32(0.0))))
        section = jnp.where(live_slots, score - rank_norm + gen_logit - norm_value + math.log(ITEMS), jnp.float32(0.0))
        chosen = jnp.sum(jnp.where(positions == logged_index, section, jnp.float32(0.0)))
        weight = chosen + jnp.log(list_length.astype(jnp.float32)) - jnp.log(propensity.astype(jnp.float32) / 1024.0)
        return section, weight

    section_logp, log_weight = lax.map(per_context, (query, context_features, candidates, lengths, log_norm, logged_slot, logging_prop))
    return section_logp, log_weight
```

```python
import functools
import math

import jax
import jax.numpy as jnp
from jax import lax
from jax.experimental import pallas as pl
from jax.experimental.pallas import tpu as pltpu
from jax.sharding import PartitionSpec as P

F32 = jnp.float32
BF16 = jnp.bfloat16
LANES = 128
NT = (((1,), (1,)), ((), ()))
NN = (((1,), (0,)), ((), ()))
TN = (((0,), (0,)), ((), ()))


def round_up(value, step):
    return (value + step - 1) // step * step


def dot(left, right, dims):
    return lax.dot_general(left, right, dims, preferred_element_type=F32)


def silu(v):
    half = v * 0.5
    return half + half * jnp.tanh(half)


def kernel(
    dp_size,
    item_size,
    cap,
    query_ref,
    feature_ref,
    cand_ref,
    length_ref,
    slot_ref,
    prop_ref,
    table_hbm,
    first_hbm,
    second_hbm,
    score_ref,
    section_ref,
    weight_ref,
    table,
    first,
    second_w,
    send1,
    recv1,
    send2,
    recv2,
    load_sem,
    send_sem,
    recv_sem,
    own_sem,
):
    n = dp_size * item_size
    item_rows, width = table.shape
    slots = cand_ref.shape[1]
    feature_width = feature_ref.shape[1]
    hidden_width = first.shape[1]
    gen_at = round_up(cap, 8)
    max_at = 2 * gen_at
    me = lax.axis_index("dp") * item_size + lax.axis_index("item")

    loads = [
        pltpu.make_async_copy(first_hbm, first, load_sem.at[0]),
        pltpu.make_async_copy(table_hbm, table, load_sem.at[1]),
        pltpu.make_async_copy(second_hbm, second_w, load_sem.at[2]),
    ]
    for load in loads:
        load.start()

    def device(j):
        peer = lax.rem(me + j, n)
        return peer, {"dp": lax.div(peer, item_size), "item": lax.rem(peer, item_size)}

    barrier = pltpu.get_barrier_semaphore()

    @pl.loop(1, n)
    def greet(j):
        peer, where = device(j)
        pl.semaphore_signal(barrier, inc=1, device_id=where, device_id_type=pl.DeviceIdType.MESH)

    ids = cand_ref[...]
    holder = lax.div(ids, item_rows)
    local = ids - holder * item_rows
    high = lax.div(local, LANES).astype(F32)
    low = lax.rem(local, LANES).astype(F32)
    held = (lax.broadcasted_iota(jnp.int32, (n, slots), 0) == holder).astype(F32)
    blocks = slots // LANES
    stacked = jnp.concatenate(
        [held[:, b * LANES : (b + 1) * LANES] for b in range(blocks)], axis=0
    ).astype(BF16)
    before = (
        lax.broadcasted_iota(jnp.int32, (LANES, LANES), 0)
        < lax.broadcasted_iota(jnp.int32, (LANES, LANES), 1)
    ).astype(F32)
    counter = jnp.concatenate([before, jnp.ones((LANES, LANES), F32)], axis=1).astype(BF16)
    counts = dot(stacked, counter, NN)
    total = jnp.zeros((n, LANES), F32)
    rank_parts = []
    for b in range(blocks):
        here = counts[b * n : (b + 1) * n]
        place = here[:, :LANES] + total
        rank_parts.append(
            jnp.sum(held[:, b * LANES : (b + 1) * LANES] * place, axis=0, keepdims=True)
        )
        total = total + here[:, LANES:]
    rank = jnp.concatenate(rank_parts, axis=1)
    at_rank = (
        lax.broadcasted_iota(jnp.int32, (LANES, slots), 0).astype(F32) == rank
    ).astype(F32)
    parts = jnp.concatenate([held * high, held * low], axis=0).astype(BF16)
    asked = dot(parts, at_rank.astype(BF16), NT)
    asked = asked[:n] * float(LANES) + asked[n:]

    loads[0].wait()
    context_part = dot(feature_ref[...], first[:feature_width, :], NN)
    send1[:, 0, :width] = jnp.broadcast_to(query_ref[...].astype(F32), (n, width))
    send1[:, 0, width : width + hidden_width] = jnp.broadcast_to(context_part, (n, hidden_width))
    send1[:, 0, width + hidden_width :] = asked

    pl.semaphore_wait(barrier, n - 1)

    def exchange(source, target, index):
        @pl.loop(1, n)
        def send(j):
            peer, where = device(j)
            pltpu.make_async_remote_copy(
                src_ref=source.at[pl.ds(peer, 1)],
                dst_ref=target.at[pl.ds(me, 1)],
                send_sem=send_sem.at[index],
                recv_sem=recv_sem.at[index],
                device_id=where,
                device_id_type=pl.DeviceIdType.MESH,
            ).start()

        own = pltpu.make_async_copy(
            source.at[pl.ds(me, 1)], target.at[pl.ds(me, 1)], own_sem.at[index]
        )
        own.start()
        own.wait()

    def arrived(target, index):
        pltpu.make_async_copy(
            target.at[pl.ds(0, n - 1)], target.at[pl.ds(0, n - 1)], recv_sem.at[index]
        ).wait()

    def sent(source, index):
        pltpu.make_async_copy(
            source.at[pl.ds(0, n - 1)], source.at[pl.ds(0, n - 1)], send_sem.at[index]
        ).wait()

    exchange(send1, recv1, 0)
    loads[1].wait()
    loads[2].wait()
    arrived(recv1, 0)

    queries = recv1[:, 0, :width]
    logits = dot(queries.astype(BF16), table[...], NT)
    local_max = jnp.max(logits, axis=1, keepdims=True)
    local_sum = jnp.sum(jnp.exp(logits - local_max), axis=1, keepdims=True)

    lane = lax.broadcasted_iota(jnp.int32, (n, LANES), 1)
    result = jnp.where(lane == max_at, local_max, 0.0)
    result = jnp.where(lane == max_at + 1, local_sum, result)
    score_rows = jnp.broadcast_to(score_ref[...], (LANES, hidden_width))
    item_iota = lax.broadcasted_iota(jnp.int32, (n, item_rows), 1).astype(F32)
    group = max(1, 256 // n)
    for start in range(0, cap, group):
        ranks = range(start, min(start + group, cap))
        picks = []
        for r in ranks:
            index = recv1[:, 0, width + hidden_width + r : width + hidden_width + r + 1]
            picks.append((item_iota == index).astype(F32).astype(BF16))
        rows = dot(jnp.concatenate(picks, axis=0), table[...], NN)
        item_part = dot(rows.astype(BF16), first[feature_width:, :], NN)
        context = recv1[:, 0, width : width + hidden_width]
        hidden = silu(item_part + jnp.concatenate([context] * len(ranks), axis=0)).astype(BF16)
        second = silu(dot(hidden, second_w[...], NN)).astype(BF16)
        score = dot(second, score_rows, NT)
        for place, r in enumerate(ranks):
            mine = slice(place * n, (place + 1) * n)
            gen = jnp.sum(rows[mine] * queries, axis=1, keepdims=True)
            result = jnp.where(lane == r, score[mine], result)
            result = jnp.where(lane == gen_at + r, gen, result)
    send2[:, 0, :] = result

    exchange(send2, recv2, 1)
    sent(send1, 0)
    arrived(recv2, 1)

    back = recv2[:, 0, :]
    top = back.astype(BF16)
    rest = back - top.astype(F32)
    middle = rest.astype(BF16)
    bottom = (rest - middle.astype(F32)).astype(BF16)
    pieces = jnp.concatenate([top.astype(F32), middle.astype(F32), bottom.astype(F32)], axis=0)
    held_bf = held.astype(BF16)
    spread = dot(
        pieces.astype(BF16).T, jnp.concatenate([held_bf, held_bf, held_bf], axis=0), NN
    )
    score = jnp.sum(at_rank[:gen_at] * spread[:gen_at], axis=0, keepdims=True)
    gen = jnp.sum(at_rank[:gen_at] * spread[gen_at : 2 * gen_at], axis=0, keepdims=True)

    maxima = back[:, max_at : max_at + 1]
    sums = back[:, max_at + 1 : max_at + 2]
    peak = jnp.max(maxima, axis=0, keepdims=True)
    log_norm = peak + jnp.log(jnp.sum(sums * jnp.exp(maxima - peak), axis=0, keepdims=True))

    length = length_ref[0]
    position = lax.broadcasted_iota(jnp.int32, (1, slots), 1)
    live = position < length
    masked = jnp.where(live, score, -1e30)
    rank_peak = jnp.max(masked, axis=1, keepdims=True)
    rank_norm = rank_peak + jnp.log(
        jnp.sum(jnp.where(live, jnp.exp(masked - rank_peak), 0.0), axis=1, keepdims=True)
    )
    section = jnp.where(
        live, score - rank_norm + gen - log_norm + math.log(item_rows * n), 0.0
    )
    chosen = jnp.sum(jnp.where(position == slot_ref[0], section, 0.0), axis=1, keepdims=True)
    length_row = jnp.broadcast_to(length, (1, LANES)).astype(F32)
    prop_row = jnp.broadcast_to(prop_ref[0], (1, LANES)).astype(F32) / 1024.0
    section_ref[...] = section
    weight_ref[...] = chosen + (jnp.log(length_row) - jnp.log(prop_row))[:, :1]
    sent(send2, 1)


def solution(mesh):
    dp_size, item_size = mesh.shape["dp"], mesh.shape["item"]
    n = dp_size * item_size

    def body(
        query,
        item_table,
        context_features,
        candidates,
        lengths,
        logged_slot,
        logging_prop,
        w_first,
        w_second,
        w_score,
    ):
        slots = candidates.shape[1]
        cap = max(2, 3 * slots // (2 * n))
        width = query.shape[1]
        hidden_width = w_first.shape[1]
        message = width + hidden_width + LANES
        vmem = pl.BlockSpec(memory_space=pltpu.VMEM)
        smem = pl.BlockSpec(memory_space=pltpu.SMEM)
        hbm = pl.BlockSpec(memory_space=pl.ANY)
        section, weight = pl.pallas_call(
            functools.partial(kernel, dp_size, item_size, cap),
            out_shape=(
                jax.ShapeDtypeStruct((1, slots), F32),
                jax.ShapeDtypeStruct((1, 1), F32),
            ),
            in_specs=[vmem, vmem, vmem, smem, smem, smem, hbm, hbm, hbm, vmem],
            out_specs=(vmem, vmem),
            scratch_shapes=[
                pltpu.VMEM(item_table.shape, BF16),
                pltpu.VMEM(w_first.shape, BF16),
                pltpu.VMEM(w_second.shape, BF16),
                pltpu.VMEM((n, 1, message), F32),
                pltpu.VMEM((n, 1, message), F32),
                pltpu.VMEM((n, 1, LANES), F32),
                pltpu.VMEM((n, 1, LANES), F32),
                pltpu.SemaphoreType.DMA((3,)),
                pltpu.SemaphoreType.DMA((2,)),
                pltpu.SemaphoreType.DMA((2,)),
                pltpu.SemaphoreType.DMA((2,)),
            ],
            compiler_params=pltpu.CompilerParams(collective_id=0, has_side_effects=True),
            name="propensity",
        )(
            query,
            context_features,
            candidates,
            lengths,
            logged_slot,
            logging_prop,
            item_table,
            w_first,
            w_second,
            w_score.reshape(1, -1),
        )
        return section, weight.reshape(-1)

    split = P(("dp", "item"))
    rows = P(("dp", "item"), None)
    return jax.shard_map(
        body,
        mesh=mesh,
        in_specs=(rows, rows, rows, rows, split, split, split, P(), P(), P()),
        out_specs=(rows, split),
        check_vma=False,
    )
```

```python
import functools
import math

import jax
import jax.numpy as jnp
from jax import lax
from jax.experimental import pallas as pl
from jax.experimental.pallas import tpu as pltpu
from jax.sharding import PartitionSpec as P

F32 = jnp.float32
BF16 = jnp.bfloat16
LANES = 128
NT = (((1,), (1,)), ((), ()))
NN = (((1,), (0,)), ((), ()))
TN = (((0,), (0,)), ((), ()))


def round_up(value, step):
    return (value + step - 1) // step * step


def dot(left, right, dims):
    return lax.dot_general(left, right, dims, preferred_element_type=F32)


def silu(v):
    half = v * 0.5
    return half + half * jnp.tanh(half)


def kernel(
    dp_size,
    item_size,
    groups,
    cap,
    query_hbm,
    feature_hbm,
    cand_hbm,
    length_hbm,
    slot_hbm,
    prop_hbm,
    table_hbm,
    first_hbm,
    second_hbm,
    score_hbm,
    section_ref,
    weight_ref,
    query_ref,
    feature_ref,
    cand_ref,
    length_ref,
    slot_ref,
    prop_ref,
    score_ref,
    table,
    first,
    second_w,
    send1,
    recv1,
    send2,
    recv2,
    load_sem,
    send_sem,
    arrive_sem,
    return_sem,
    own_sem,
):
    n = dp_size * item_size
    item_rows, width = table.shape
    slots = cand_ref.shape[1]
    feature_width = feature_ref.shape[1]
    hidden_width = first.shape[1]
    gen_at = round_up(cap, 8)
    max_at = 2 * gen_at
    dp_me, item_me = lax.axis_index("dp"), lax.axis_index("item")
    me = dp_me * item_size + item_me
    run = item_size // groups
    members = dp_size * run
    run_me = lax.div(item_me, run)
    member_me = dp_me * run + lax.rem(item_me, run)

    def device(offset, member):
        dp = lax.div(member, run)
        item = lax.rem(run_me + offset, groups) * run + lax.rem(member, run)
        return dp * item_size + item, {"dp": dp, "item": item}

    def each_peer(offset, act):
        @pl.loop(1 if offset == 0 else 0, members)
        def visit(j):
            member = lax.rem(member_me + j, members)
            peer, where = device(offset, member)
            act(member, peer, where)

    barrier = pltpu.get_barrier_semaphore()

    def greet(member, peer, where):
        pl.semaphore_signal(barrier, inc=1, device_id=where, device_id_type=pl.DeviceIdType.MESH)

    far_first = sorted(range(groups), key=lambda g: -min(g, groups - g))
    for offset in far_first:
        each_peer(offset, greet)

    loads = [
        pltpu.make_async_copy(source, target, load_sem.at[i])
        for i, (source, target) in enumerate(
            [
                (cand_hbm, cand_ref),
                (query_hbm, query_ref),
                (feature_hbm, feature_ref),
                (first_hbm, first),
                (table_hbm, table),
                (second_hbm, second_w),
                (score_hbm, score_ref),
                (length_hbm, length_ref),
                (slot_hbm, slot_ref),
                (prop_hbm, prop_ref),
            ]
        )
    ]
    for load in loads:
        load.start()
    loads[0].wait()

    ids = cand_ref[...]
    holder = lax.div(ids, item_rows)
    local = ids - holder * item_rows
    high = lax.div(local, LANES).astype(F32)
    low = lax.rem(local, LANES).astype(F32)
    held = (lax.broadcasted_iota(jnp.int32, (n, slots), 0) == holder).astype(F32)
    blocks = slots // LANES
    stacked = jnp.concatenate(
        [held[:, b * LANES : (b + 1) * LANES] for b in range(blocks)], axis=0
    ).astype(BF16)
    before = (
        lax.broadcasted_iota(jnp.int32, (LANES, LANES), 0)
        < lax.broadcasted_iota(jnp.int32, (LANES, LANES), 1)
    ).astype(F32)
    counter = jnp.concatenate([before, jnp.ones((LANES, LANES), F32)], axis=1).astype(BF16)
    counts = dot(stacked, counter, NN)
    total = jnp.zeros((n, LANES), F32)
    rank_parts = []
    for b in range(blocks):
        here = counts[b * n : (b + 1) * n]
        place = here[:, :LANES] + total
        rank_parts.append(
            jnp.sum(held[:, b * LANES : (b + 1) * LANES] * place, axis=0, keepdims=True)
        )
        total = total + here[:, LANES:]
    rank = jnp.concatenate(rank_parts, axis=1)
    at_rank = (
        lax.broadcasted_iota(jnp.int32, (LANES, slots), 0).astype(F32) == rank
    ).astype(F32)
    parts = jnp.concatenate([held * high, held * low], axis=0).astype(BF16)
    asked = dot(parts, at_rank.astype(BF16), NT)
    asked = asked[:n] * float(LANES) + asked[n:]

    for load in loads[1:4]:
        load.wait()
    context_part = dot(feature_ref[...], first[:feature_width, :], NN)
    send1[:, 0, :width] = jnp.broadcast_to(query_ref[...].astype(F32), (n, width))
    send1[:, 0, width : width + hidden_width] = jnp.broadcast_to(context_part, (n, hidden_width))
    send1[:, 0, width + hidden_width :] = asked

    pl.semaphore_wait(barrier, n - 1)

    def ask(offset):
        seen = (groups - offset) % groups

        def act(member, peer, where):
            pltpu.make_async_remote_copy(
                src_ref=send1.at[pl.ds(peer, 1)],
                dst_ref=recv1.at[pl.ds(seen * members + member_me, 1)],
                send_sem=send_sem.at[0],
                recv_sem=arrive_sem.at[seen],
                device_id=where,
                device_id_type=pl.DeviceIdType.MESH,
            ).start()

        each_peer(offset, act)

    def give_back(offset):
        def act(member, peer, where):
            pltpu.make_async_remote_copy(
                src_ref=send2.at[pl.ds(offset * members + member, 1)],
                dst_ref=recv2.at[pl.ds(me, 1)],
                send_sem=send_sem.at[1],
                recv_sem=return_sem,
                device_id=where,
                device_id_type=pl.DeviceIdType.MESH,
            ).start()

        each_peer(offset, act)

    def wait_rows(buffer, count, semaphore):
        rows = buffer.at[pl.ds(0, count)]
        pltpu.make_async_copy(rows, rows, semaphore).wait()

    own_ask = pltpu.make_async_copy(
        send1.at[pl.ds(me, 1)], recv1.at[pl.ds(member_me, 1)], own_sem.at[0]
    )
    own_ask.start()
    for offset in far_first:
        ask(offset)
    for load in loads[4:]:
        load.wait()
    own_ask.wait()

    lane = lax.broadcasted_iota(jnp.int32, (members, LANES), 1)
    score_rows = jnp.broadcast_to(score_ref[...].reshape(1, hidden_width), (LANES, hidden_width))
    item_iota = lax.broadcasted_iota(jnp.int32, (members, item_rows), 1).astype(F32)

    def rank_group(group):
        rows_here = pl.ds(group * members, members)
        query = recv1[rows_here, 0, :width]
        context = recv1[rows_here, 0, width : width + hidden_width]
        wanted = recv1[rows_here, 0, width + hidden_width :]
        picks = [
            (item_iota == wanted[:, r : r + 1]).astype(F32) for r in range(cap)
        ]
        rows = dot(jnp.concatenate(picks, axis=0).astype(BF16), table[...], NN)
        item_part = dot(rows.astype(BF16), first[feature_width:, :], NN)
        hidden = silu(item_part + jnp.concatenate([context] * cap, axis=0)).astype(BF16)
        second = silu(dot(hidden, second_w[...], NN)).astype(BF16)
        score = dot(second, score_rows, NT)
        result = jnp.zeros((members, LANES), F32)
        for r in range(cap):
            mine = slice(r * members, (r + 1) * members)
            gen = jnp.sum(rows[mine] * query, axis=1, keepdims=True)
            result = jnp.where(lane == r, score[mine], result)
            result = jnp.where(lane == gen_at + r, gen, result)
        return result

    def normalizers():
        logits = dot(recv1[:, 0, :width].astype(BF16), table[...], NT)
        local_max = jnp.max(logits, axis=1, keepdims=True)
        local_sum = jnp.sum(jnp.exp(logits - local_max), axis=1, keepdims=True)
        return local_max, local_sum

    order = sorted(range(groups), key=lambda g: min(g, groups - g))
    order = order[:-2] + order[:-3:-1]
    results = {}
    waited = set()

    def wait_group(group):
        if group not in waited:
            waited.add(group)
            wait_rows(recv1, members - 1 if group == 0 else members, arrive_sem.at[group])

    for group in order[:-2]:
        wait_group(group)
        results[group] = rank_group(group)
    for group in order[-2:]:
        wait_group(group)
    local_max, local_sum = normalizers()

    def finish(group):
        mine = slice(group * members, (group + 1) * members)
        result = jnp.where(lane == max_at, local_max[mine], results[group])
        result = jnp.where(lane == max_at + 1, local_sum[mine], result)
        send2[pl.ds(group * members, members), 0, :] = result
        give_back(group)

    for group in reversed(order[:-2]):
        finish(group)
    own_back = pltpu.make_async_copy(
        send2.at[pl.ds(member_me, 1)], recv2.at[pl.ds(me, 1)], own_sem.at[1]
    )
    own_back.start()
    for group in order[-2:]:
        results[group] = rank_group(group)
        finish(group)
    own_back.wait()
    wait_rows(send1, n - 1, send_sem.at[0])
    wait_rows(recv2, n - 1, return_sem)

    back = recv2[:, 0, :]
    top = back.astype(BF16)
    rest = back - top.astype(F32)
    middle = rest.astype(BF16)
    bottom = (rest - middle.astype(F32)).astype(BF16)
    pieces = jnp.concatenate([top.astype(F32), middle.astype(F32), bottom.astype(F32)], axis=0)
    held_bf = held.astype(BF16)
    spread = dot(
        pieces.astype(BF16).T, jnp.concatenate([held_bf, held_bf, held_bf], axis=0), NN
    )
    score = jnp.sum(at_rank[:gen_at] * spread[:gen_at], axis=0, keepdims=True)
    gen = jnp.sum(at_rank[:gen_at] * spread[gen_at : 2 * gen_at], axis=0, keepdims=True)

    maxima = back[:, max_at : max_at + 1]
    sums = back[:, max_at + 1 : max_at + 2]
    peak = jnp.max(maxima, axis=0, keepdims=True)
    log_norm = peak + jnp.log(jnp.sum(sums * jnp.exp(maxima - peak), axis=0, keepdims=True))

    length = length_ref[0]
    position = lax.broadcasted_iota(jnp.int32, (1, slots), 1)
    live = position < length
    masked = jnp.where(live, score, -1e30)
    rank_peak = jnp.max(masked, axis=1, keepdims=True)
    rank_norm = rank_peak + jnp.log(
        jnp.sum(jnp.where(live, jnp.exp(masked - rank_peak), 0.0), axis=1, keepdims=True)
    )
    section = jnp.where(
        live, score - rank_norm + gen - log_norm + math.log(item_rows * n), 0.0
    )
    chosen = jnp.sum(jnp.where(position == slot_ref[0], section, 0.0), axis=1, keepdims=True)
    length_row = jnp.broadcast_to(length, (1, LANES)).astype(F32)
    prop_row = jnp.broadcast_to(prop_ref[0], (1, LANES)).astype(F32) / 1024.0
    section_ref[...] = section
    weight_ref[...] = chosen + (jnp.log(length_row) - jnp.log(prop_row))[:, :1]
    wait_rows(send2, n - 1, send_sem.at[1])


def solution(mesh):
    dp_size, item_size = mesh.shape["dp"], mesh.shape["item"]
    n = dp_size * item_size

    def body(
        query,
        item_table,
        context_features,
        candidates,
        lengths,
        logged_slot,
        logging_prop,
        w_first,
        w_second,
        w_score,
    ):
        slots = candidates.shape[1]
        cap = max(2, 3 * slots // (2 * n))
        width = query.shape[1]
        hidden_width = w_first.shape[1]
        message = width + hidden_width + LANES
        vmem = pl.BlockSpec(memory_space=pltpu.VMEM)
        groups = math.gcd(4, item_size)
        hbm = pl.BlockSpec(memory_space=pl.ANY)
        section, weight = pl.pallas_call(
            functools.partial(kernel, dp_size, item_size, groups, cap),
            out_shape=(
                pltpu.VMEM((1, slots), F32),
                pltpu.VMEM((1, 1), F32),
            ),
            in_specs=[pl.BlockSpec(memory_space=pltpu.HBM)] * 10,
            out_specs=(vmem, vmem),
            scratch_shapes=[
                pltpu.VMEM(query.shape, BF16),
                pltpu.VMEM(context_features.shape, BF16),
                pltpu.VMEM(candidates.shape, jnp.int32),
                pltpu.SMEM(lengths.shape, jnp.int32),
                pltpu.SMEM(logged_slot.shape, jnp.int32),
                pltpu.SMEM(logging_prop.shape, jnp.int32),
                pltpu.VMEM(w_score.shape, BF16),
                pltpu.VMEM(item_table.shape, BF16),
                pltpu.VMEM(w_first.shape, BF16),
                pltpu.VMEM(w_second.shape, BF16),
                pltpu.VMEM((n, 1, message), F32),
                pltpu.VMEM((n, 1, message), F32),
                pltpu.VMEM((n, 1, LANES), F32),
                pltpu.VMEM((n, 1, LANES), F32),
                pltpu.SemaphoreType.DMA((10,)),
                pltpu.SemaphoreType.DMA((2,)),
                pltpu.SemaphoreType.DMA((groups,)),
                pltpu.SemaphoreType.DMA,
                pltpu.SemaphoreType.DMA((2,)),
            ],
            compiler_params=pltpu.CompilerParams(collective_id=0, has_side_effects=True),
            name="propensity",
        )(
            query,
            context_features,
            candidates,
            lengths,
            logged_slot,
            logging_prop,
            item_table,
            w_first,
            w_second,
            w_score,
        )
        return section, weight.reshape(-1)

    split = P(("dp", "item"))
    rows = P(("dp", "item"), None)
    return jax.shard_map(
        body,
        mesh=mesh,
        in_specs=(rows, rows, rows, rows, split, split, split, P(), P(), P()),
        out_specs=(rows, split),
        check_vma=False,
    )
```

```python
import functools
import math

import jax
import jax.numpy as jnp
from jax import lax
from jax.experimental import pallas as pl
from jax.experimental.pallas import tpu as pltpu
from jax.sharding import PartitionSpec as P

F32 = jnp.float32
BF16 = jnp.bfloat16
LANES = 128
NT = (((1,), (1,)), ((), ()))
NN = (((1,), (0,)), ((), ()))
TN = (((0,), (0,)), ((), ()))


def round_up(value, step):
    return (value + step - 1) // step * step


def dot(left, right, dims):
    return lax.dot_general(left, right, dims, preferred_element_type=F32)


def silu(v):
    half = v * 0.5
    return half + half * jnp.tanh(half)


def kernel(
    dp_size,
    item_size,
    groups,
    cap,
    query_hbm,
    feature_hbm,
    cand_hbm,
    scalar_hbm,
    table_hbm,
    first_hbm,
    second_hbm,
    score_hbm,
    section_ref,
    weight_ref,
    query_ref,
    feature_ref,
    cand_ref,
    scalar_ref,
    score_ref,
    table,
    first,
    second_w,
    send1,
    recv1,
    send2,
    recv2,
    load_sem,
    send_sem,
    arrive_sem,
    return_sem,
    own_sem,
    items,
    found,
    wanted_v,
    wanted_at,
    index_sem,
):
    n = dp_size * item_size
    item_rows, width = table.shape
    slots = cand_ref.shape[1]
    feature_width = feature_ref.shape[1]
    hidden_width = first.shape[1]
    gen_at = round_up(cap, 8)
    max_at = 2 * gen_at
    dp_me, item_me = lax.axis_index("dp"), lax.axis_index("item")
    me = dp_me * item_size + item_me
    run = item_size // groups
    members = dp_size * run
    run_me = lax.div(item_me, run)
    member_me = dp_me * run + lax.rem(item_me, run)

    def device(offset, member):
        dp = lax.div(member, run)
        item = lax.rem(run_me + offset, groups) * run + lax.rem(member, run)
        return dp * item_size + item, {"dp": dp, "item": item}

    def each_peer(offset, act):
        @pl.loop(1 if offset == 0 else 0, members)
        def visit(j):
            member = lax.rem(member_me + j, members)
            peer, where = device(offset, member)
            act(member, peer, where)

    barrier = pltpu.get_barrier_semaphore()

    def greet(member, peer, where):
        pl.semaphore_signal(barrier, inc=1, device_id=where, device_id_type=pl.DeviceIdType.MESH)

    far_first = sorted(range(groups), key=lambda g: -min(g, groups - g))
    for offset in far_first:
        each_peer(offset, greet)

    loads = [
        pltpu.make_async_copy(source, target, load_sem.at[i])
        for i, (source, target) in enumerate(
            [
                (cand_hbm, cand_ref),
                (query_hbm, query_ref),
                (feature_hbm, feature_ref),
                (first_hbm, first),
                (table_hbm, table),
                (second_hbm, second_w),
                (score_hbm, score_ref),
                (scalar_hbm, scalar_ref),
            ]
        )
    ]
    for load in loads:
        load.start()
    loads[0].wait()

    ids = cand_ref[...]
    holder = lax.div(ids, item_rows)
    local = ids - holder * item_rows
    high = lax.div(local, LANES).astype(F32)
    low = lax.rem(local, LANES).astype(F32)
    held = (lax.broadcasted_iota(jnp.int32, (n, slots), 0) == holder).astype(F32)
    blocks = slots // LANES
    stacked = jnp.concatenate(
        [held[:, b * LANES : (b + 1) * LANES] for b in range(blocks)], axis=0
    ).astype(BF16)
    before = (
        lax.broadcasted_iota(jnp.int32, (LANES, LANES), 0)
        < lax.broadcasted_iota(jnp.int32, (LANES, LANES), 1)
    ).astype(F32)
    counter = jnp.concatenate([before, jnp.ones((LANES, LANES), F32)], axis=1).astype(BF16)
    counts = dot(stacked, counter, NN)
    total = jnp.zeros((n, LANES), F32)
    rank_parts = []
    for b in range(blocks):
        here = counts[b * n : (b + 1) * n]
        place = here[:, :LANES] + total
        rank_parts.append(
            jnp.sum(held[:, b * LANES : (b + 1) * LANES] * place, axis=0, keepdims=True)
        )
        total = total + here[:, LANES:]
    rank = jnp.concatenate(rank_parts, axis=1)
    at_rank = (
        lax.broadcasted_iota(jnp.int32, (LANES, slots), 0).astype(F32) == rank
    ).astype(F32)
    parts = jnp.concatenate([held * high, held * low], axis=0).astype(BF16)
    asked = dot(parts, at_rank.astype(BF16), NT)
    asked = asked[:n] * float(LANES) + asked[n:]

    for load in loads[1:4]:
        load.wait()
    context_part = dot(feature_ref[...], first[:feature_width, :], NN)
    send1[:, 0, :width] = jnp.broadcast_to(query_ref[...].astype(F32), (n, width))
    send1[:, 0, width : width + hidden_width] = jnp.broadcast_to(context_part, (n, hidden_width))
    send1[:, 0, width + hidden_width :] = asked

    pl.semaphore_wait(barrier, n - 1)

    def ask(offset):
        seen = (groups - offset) % groups

        def act(member, peer, where):
            pltpu.make_async_remote_copy(
                src_ref=send1.at[pl.ds(peer, 1)],
                dst_ref=recv1.at[pl.ds(seen * members + member_me, 1)],
                send_sem=send_sem.at[0],
                recv_sem=arrive_sem.at[seen],
                device_id=where,
                device_id_type=pl.DeviceIdType.MESH,
            ).start()

        each_peer(offset, act)

    def give_back(offset):
        def act(member, peer, where):
            pltpu.make_async_remote_copy(
                src_ref=send2.at[pl.ds(offset * members + member, 1)],
                dst_ref=recv2.at[pl.ds(me, 1)],
                send_sem=send_sem.at[1],
                recv_sem=return_sem,
                device_id=where,
                device_id_type=pl.DeviceIdType.MESH,
            ).start()

        each_peer(offset, act)

    def wait_rows(buffer, count, semaphore):
        rows = buffer.at[pl.ds(0, count)]
        pltpu.make_async_copy(rows, rows, semaphore).wait()

    own_ask = pltpu.make_async_copy(
        send1.at[pl.ds(me, 1)], recv1.at[pl.ds(member_me, 1)], own_sem.at[0]
    )
    own_ask.start()
    for offset in far_first:
        ask(offset)
    for load in loads[4:]:
        load.wait()
    own_ask.wait()

    lane = lax.broadcasted_iota(jnp.int32, (members, LANES), 1)
    score_rows = jnp.broadcast_to(score_ref[...].reshape(1, hidden_width), (LANES, hidden_width))
    hidden_tiles = hidden_width // LANES
    tall = items.shape[1]
    step = math.gcd(256, item_rows)

    @pl.loop(0, item_rows // step)
    def project(i):
        part = pl.ds(pl.multiple_of(i * step, step), step)
        block = table[part]
        projected = dot(block, first[feature_width:, :], NN)
        for j in range(hidden_tiles):
            items[part, j] = projected[:, j * LANES : (j + 1) * LANES]
        for j in range(width // LANES):
            items[part, hidden_tiles + j] = block[:, j * LANES : (j + 1) * LANES].astype(F32)


    def to_scalar(group):
        rows_here = pl.ds(group * members, members)
        return pltpu.make_async_copy(
            wanted_v.at[rows_here], wanted_at.at[rows_here], index_sem.at[group]
        )

    def rank_group(group):
        rows_here = pl.ds(group * members, members)
        query = recv1[rows_here, 0, :width]
        context = recv1[rows_here, 0, width : width + hidden_width]
        to_scalar(group).wait()
        for r in range(cap):
            for c in range(members):
                at = jnp.clip(wanted_at[group * members + c, 0, r], 0, item_rows - 1)
                place = (group * cap + r) * members + c
                found[pl.ds(place * tall, tall)] = items[at]
        count = cap * members

        def found_tile(j):
            return found[pl.ds(group * count * tall + j, count, stride=tall), :]

        item_part = jnp.concatenate([found_tile(j) for j in range(hidden_tiles)], axis=1)
        rows = jnp.concatenate(
            [found_tile(hidden_tiles + j) for j in range(width // LANES)], axis=1
        )
        hidden = silu(item_part + jnp.concatenate([context] * cap, axis=0)).astype(BF16)
        second = silu(dot(hidden, second_w[...], NN)).astype(BF16)
        score = dot(second, score_rows, NT)
        result = jnp.zeros((members, LANES), F32)
        for r in range(cap):
            mine = slice(r * members, (r + 1) * members)
            gen = jnp.sum(rows[mine] * query, axis=1, keepdims=True)
            result = jnp.where(lane == r, score[mine], result)
            result = jnp.where(lane == gen_at + r, gen, result)
        return result

    def normalizers():
        logits = dot(recv1[:, 0, :width].astype(BF16), table[...], NT)
        local_max = jnp.max(logits, axis=1, keepdims=True)
        local_sum = jnp.sum(jnp.exp(logits - local_max), axis=1, keepdims=True)
        return local_max, local_sum

    order = sorted(range(groups), key=lambda g: min(g, groups - g))
    order = order[:-2] + order[:-3:-1]
    results = {}
    waited = set()

    def wait_group(group):
        if group not in waited:
            waited.add(group)
            wait_rows(recv1, members - 1 if group == 0 else members, arrive_sem.at[group])
            rows_here = pl.ds(group * members, members)
            wanted_v[rows_here] = recv1[rows_here, :, width + hidden_width :].astype(jnp.int32)
            to_scalar(group).start()

    for group in order[:-2]:
        wait_group(group)
        results[group] = rank_group(group)
    for group in order[-2:]:
        wait_group(group)
    local_max, local_sum = normalizers()

    def finish(group):
        mine = slice(group * members, (group + 1) * members)
        result = jnp.where(lane == max_at, local_max[mine], results[group])
        result = jnp.where(lane == max_at + 1, local_sum[mine], result)
        send2[pl.ds(group * members, members), 0, :] = result
        give_back(group)

    for group in reversed(order[:-2]):
        finish(group)
    own_back = pltpu.make_async_copy(
        send2.at[pl.ds(member_me, 1)], recv2.at[pl.ds(me, 1)], own_sem.at[1]
    )
    own_back.start()
    for group in order[-2:]:
        results[group] = rank_group(group)
        finish(group)
    own_back.wait()
    wait_rows(send1, n - 1, send_sem.at[0])
    wait_rows(recv2, n - 1, return_sem)

    back = recv2[:, 0, :]
    top = back.astype(BF16)
    rest = back - top.astype(F32)
    middle = rest.astype(BF16)
    bottom = (rest - middle.astype(F32)).astype(BF16)
    pieces = jnp.concatenate([top.astype(F32), middle.astype(F32), bottom.astype(F32)], axis=0)
    held_bf = held.astype(BF16)
    spread = dot(
        pieces.astype(BF16).T, jnp.concatenate([held_bf, held_bf, held_bf], axis=0), NN
    )
    score = jnp.sum(at_rank[:gen_at] * spread[:gen_at], axis=0, keepdims=True)
    gen = jnp.sum(at_rank[:gen_at] * spread[gen_at : 2 * gen_at], axis=0, keepdims=True)

    maxima = back[:, max_at : max_at + 1]
    sums = back[:, max_at + 1 : max_at + 2]
    peak = jnp.max(maxima, axis=0, keepdims=True)
    log_norm = peak + jnp.log(jnp.sum(sums * jnp.exp(maxima - peak), axis=0, keepdims=True))

    length = scalar_ref[:, 0:1]
    position = lax.broadcasted_iota(jnp.int32, (1, slots), 1)
    live = position < length
    masked = jnp.where(live, score, -1e30)
    rank_peak = jnp.max(masked, axis=1, keepdims=True)
    rank_norm = rank_peak + jnp.log(
        jnp.sum(jnp.where(live, jnp.exp(masked - rank_peak), 0.0), axis=1, keepdims=True)
    )
    section = jnp.where(
        live, score - rank_norm + gen - log_norm + math.log(item_rows * n), 0.0
    )
    chosen = jnp.sum(jnp.where(position == scalar_ref[:, 1:2], section, 0.0), axis=1, keepdims=True)
    prop = scalar_ref[:, 2:3].astype(F32) / 1024.0
    section_ref[...] = section
    weight_ref[...] = chosen + jnp.log(length.astype(F32)) - jnp.log(prop)
    wait_rows(send2, n - 1, send_sem.at[1])


def solution(mesh):
    dp_size, item_size = mesh.shape["dp"], mesh.shape["item"]
    n = dp_size * item_size

    def body(
        query,
        item_table,
        context_features,
        candidates,
        lengths,
        logged_slot,
        logging_prop,
        w_first,
        w_second,
        w_score,
    ):
        slots = candidates.shape[1]
        cap = max(2, 3 * slots // (2 * n))
        width = query.shape[1]
        hidden_width = w_first.shape[1]
        message = width + hidden_width + LANES
        tall = round_up((width + hidden_width) // LANES, 8)
        vmem = pl.BlockSpec(memory_space=pltpu.VMEM)
        groups = math.gcd(4, item_size)
        lane = lax.broadcasted_iota(jnp.int32, (1, LANES), 1)
        scalars = jnp.where(lane == 0, lengths, jnp.where(lane == 1, logged_slot, logging_prop))
        section, weight = pl.pallas_call(
            functools.partial(kernel, dp_size, item_size, groups, cap),
            out_shape=(
                pltpu.VMEM((1, slots), F32),
                pltpu.VMEM((1, 1), F32),
            ),
            in_specs=[pl.BlockSpec(memory_space=pltpu.HBM)] * 8,
            out_specs=(vmem, vmem),
            scratch_shapes=[
                pltpu.VMEM(query.shape, BF16),
                pltpu.VMEM(context_features.shape, BF16),
                pltpu.VMEM(candidates.shape, jnp.int32),
                pltpu.VMEM((1, LANES), jnp.int32),
                pltpu.VMEM(w_score.shape, BF16),
                pltpu.VMEM(item_table.shape, BF16),
                pltpu.VMEM(w_first.shape, BF16),
                pltpu.VMEM(w_second.shape, BF16),
                pltpu.VMEM((n, 1, message), F32),
                pltpu.VMEM((n, 1, message), F32),
                pltpu.VMEM((n, 1, LANES), F32),
                pltpu.VMEM((n, 1, LANES), F32),
                pltpu.SemaphoreType.DMA((8,)),
                pltpu.SemaphoreType.DMA((2,)),
                pltpu.SemaphoreType.DMA((groups,)),
                pltpu.SemaphoreType.DMA,
                pltpu.SemaphoreType.DMA((2,)),
                pltpu.VMEM((item_table.shape[0], tall, LANES), F32),
                pltpu.VMEM((n * cap * tall + tall, LANES), F32),
                pltpu.VMEM((n, 1, LANES), jnp.int32),
                pltpu.SMEM((n, 1, LANES), jnp.int32),
                pltpu.SemaphoreType.DMA((groups,)),
            ],
            compiler_params=pltpu.CompilerParams(collective_id=0, has_side_effects=True),
            name="propensity",
        )(
            query,
            context_features,
            candidates,
            scalars,
            item_table,
            w_first,
            w_second,
            w_score,
        )
        return section, weight.reshape(-1)

    split = P(("dp", "item"))
    rows = P(("dp", "item"), None)
    return jax.shard_map(
        body,
        mesh=mesh,
        in_specs=(rows, rows, rows, rows, split, split, split, P(), P(), P()),
        out_specs=(rows, split),
        check_vma=False,
    )
```
